512 devices in a mesh: prow: 16 (over z, core), pcol: 32 (over y, x).
Axes of the slice: x: 4, y: 8, z: 8, core: 2. Of those that a mesh axis runs over, the one named last changes fastest.
Arguments:
- slab: float32 [1024, 200704], P('pcol', 'prow'), may hold values from -6 to 6
- reflectors: float32 [2, 128, 200704], P(None, 'pcol', 'prow'), may hold values from -6 to 6
- factors: float32 [2, 128, 128], P(None, 'pcol'), as said below
Outputs:
- result: float32 [1024, 200704], P('pcol', 'prow')
The draws below stay inside these ranges and needn't reach their ends.
Inputs may be any that keep to these rules, and one draw needn't show every extreme that they name: factors[p] is upper triangular with a positive diagonal.
All inputs are finite; a program needn't handle non-finite values.
Results may differ from the reference program's by a relative error of at most 0.00013.
Values sent between devices are 32-bit elements; how exact they have to be, the bound alone decides.
A program may use at most 128 MiB of HBM per device.

```python
import math
import jax
import jax.numpy as jnp
from jax import lax

NB = 128
PANELS = 2
ORDER = 200704
SLAB = 1024


def draw_factors(key, part):
    first_key, second_key = jax.random.split(jax.random.fold_in(key, 17))
    unit = 0.3 / math.sqrt(NB * ORDER)
    diagonal = jax.random.uniform(first_key, (PANELS, NB), jnp.float32, 1.0, 2.0)
    upper = jax.random.normal(second_key, (PANELS, NB, NB), jnp.float32) * 0.1
    whole = jnp.triu(upper, 1) + diagonal[:, :, None] * jnp.eye(NB, dtype=jnp.float32)[None, :, :]
    return whole * unit


def levels(own_key, shape, cuts, smallest, high):
    factor_of, own = 1.0, jax.random.fold_in(own_key, 6)
    for axis_at, shards_of in cuts:
        heights = jnp.exp(jax.random.uniform(jax.random.fold_in(own, axis_at), (shards_of,), jnp.float32, smallest / len(cuts), high / len(cuts)))
        factor_of = factor_of * jnp.repeat(heights, shape[axis_at] // shards_of).reshape([-1 if axis == axis_at else 1 for axis in range(len(shape))])
    return factor_of


def scatter_about(own_key, shape, scale, limit, pieces=(), kind=jnp.bfloat16):
    loudness = levels(own_key, shape, pieces, -0.22, 0.18) if pieces else 1.0
    drawn = jax.random.normal(own_key, shape, jnp.float32) * scale * loudness
    return jnp.minimum(jnp.maximum(drawn, -limit), limit).astype(kind)


def setup_inputs(seed: int = 0) -> dict:
    splits = jax.random.split(jax.random.key(seed), 4)
    slab = scatter_about(splits[0], (SLAB, ORDER), 1.0, 6.0, ((0, 32), (1, 16)), jnp.float32)
    reflectors = scatter_about(splits[1], (PANELS, NB, ORDER), 1.0, 6.0, ((1, 32), (2, 16)), jnp.float32)
    factors = draw_factors(jax.random.fold_in(splits[3], 71), 0)
    return dict(slab=slab, reflectors=reflectors, factors=factors)


def reference(slab, reflectors, factors):
    current = slab
    for panel_index in range(PANELS):
        vectors = reflectors[panel_index]
        inner = jnp.dot(current, vectors.T, precision=lax.Precision.HIGHEST, preferred_element_type=jnp.float32)
        scaled = jnp.dot(inner, factors[panel_index].T, precision=lax.Precision.HIGHEST, preferred_element_type=jnp.float32)
        current = current - jnp.dot(scaled, vectors, precision=lax.Precision.HIGHEST, preferred_element_type=jnp.float32)
    return current
```

```python
import functools

import jax
import jax.numpy as jnp
from jax import lax
from jax.experimental import pallas as pl
from jax.experimental.pallas import tpu as pltpu
from jax.sharding import PartitionSpec as P

X = 4
MESH = pl.DeviceIdType.MESH
LANE = 128


def quarter_start(x):
    return pl.multiple_of((24 * x + (x + X - 1) // X) * LANE, LANE)


def dot_f32(left, right, dims):
    return lax.dot_general(
        left, right, (dims, ((), ())), precision=lax.Precision.HIGHEST, preferred_element_type=jnp.float32
    )


def dot_bf16(left, right, dims):
    return lax.dot_general(left, right, (dims, ((), ())), preferred_element_type=jnp.float32)


def split_hi_lo(value):
    hi = value.astype(jnp.bfloat16)
    lo = (value - hi.astype(jnp.float32)).astype(jnp.bfloat16)
    return hi, lo


def kernel(
    dims, s_hbm, v_hbm, t_hbm, o_hbm,
    vbuf, sbuf, bhi, blo, tmat, part, ra, qsum, rb, rc, yhi, ylo, obuf,
    vx_s, vx_r, tx_s, tx_r, sx_s, sx_r, loc, ys, yr, a_s, a_r, b_s, b_r, c_s, c_r, o_s, o_r, o_l,
):
    ny, nz, rows, width, chunks = dims
    wide = width // chunks
    pr, pc = lax.axis_index("prow"), lax.axis_index("pcol")
    x, y, z, c = lax.rem(pc, X), pc // X, pr // 2, lax.rem(pr, 2)
    m = x * 2 + c
    members = 2 * X

    def at(x_to, y_to, z_to, c_to):
        return {"prow": z_to * 2 + c_to, "pcol": y_to * X + x_to}

    def along_x(d):
        return at(lax.rem(x + d, X), y, z, c)

    def along_y(d):
        return at(x, lax.rem(y + d + ny, ny), z, c)

    def along_z(d):
        return at(x, y, lax.rem(z + d, nz), c)

    def in_group(d):
        to = lax.rem(m + d, members)
        return at(to // 2, y, z, lax.rem(to, 2))

    def remote(src, dst, send, recv, to):
        return pltpu.make_async_remote_copy(
            src_ref=src, dst_ref=dst, send_sem=send, recv_sem=recv, device_id=to, device_id_type=MESH
        )

    barrier = pltpu.get_barrier_semaphore()
    peers = [along_y(1), along_y(-1)] + [in_group(d) for d in range(1, members)] + [along_z(d) for d in range(1, nz)]
    own_start = quarter_start(x)
    local = [
        pltpu.make_async_copy(
            v_hbm.at[:, :, pl.ds(own_start, width)], vbuf.at[y, x, :, :, pl.ds(0, width)], loc.at[0]
        ),
        pltpu.make_async_copy(t_hbm, vbuf.at[y, x, :, :, pl.ds(width, LANE)], loc.at[1]),
        pltpu.make_async_copy(s_hbm.at[:, pl.ds(own_start, width)], sbuf.at[x], loc.at[2]),
    ]
    for copy in local:
        copy.start()
    for to in peers:
        pl.semaphore_signal(barrier, inc=1, device_id=to, device_id_type=MESH)
    pl.semaphore_wait(barrier, len(peers))

    v_out, t_out, s_out = {}, {}, {}
    for d in (1, 3, 2):
        start = quarter_start(lax.rem(x + d, X))
        v_out[d] = remote(
            v_hbm.at[:, :, pl.ds(start, width)], vbuf.at[y, x, :, :, pl.ds(0, width)],
            vx_s.at[d], vx_r.at[d], along_x(d),
        )
        t_out[d] = remote(t_hbm, vbuf.at[y, x, :, :, pl.ds(width, LANE)], tx_s.at[d], tx_r.at[d], along_x(d))
        v_out[d].start()
        t_out[d].start()
    for d in (1, 3, 2):
        start = quarter_start(lax.rem(x + d, X))
        s_out[d] = remote(s_hbm.at[:, pl.ds(start, width)], sbuf.at[x], sx_s.at[d], sx_r.at[d], along_x(d))
        s_out[d].start()

    def convert(row):
        keep = jnp.where(x < 2, 1.0, 0.0)
        for p in range(2):
            base = pl.multiple_of(rows * 4 + p * LANE + row * 16, 16)
            value = jnp.concatenate([vbuf[row, k, p, :, pl.ds(0, width)] for k in range(X)], axis=0)
            first = value[:, :LANE] * keep
            value = jnp.concatenate([first, value[:, LANE:]], axis=1)
            hi, lo = split_hi_lo(value)
            bhi[pl.ds(base, 16), :] = hi
            blo[pl.ds(base, 16), :] = lo

    order = (0, 1, 3, 2)
    last = {0: (0, 1), 1: (3, 2)}
    sent = []
    steps = ny // 2
    for s in range(steps + 1):
        for j in order:
            if s == 0:
                if j == 0:
                    local[0].wait()
                    local[1].wait()
                else:
                    v_out[X - j].wait_recv()
                    t_out[X - j].wait_recv()
            for way in range(2):
                sign = 1 if way == 0 else -1
                if s > 0 and (s < steps or j in last[way]):
                    row = lax.rem(y - sign * s + ny, ny)
                    slot = vbuf.at[row, lax.rem(x + j, X)]
                    remote(slot, slot, ys.at[way, s - 1, j], yr.at[way, s - 1, j], along_y(sign)).wait_recv()
                if s < steps - 1 or (s == steps - 1 and j in last[way]):
                    row = lax.rem(y - sign * s + ny, ny)
                    slot = vbuf.at[row, lax.rem(x + j, X)]
                    copy = remote(slot, slot, ys.at[way, s, j], yr.at[way, s, j], along_y(sign))
                    copy.start()
                    sent.append(copy)
        if s == 0:
            convert(y)
        elif s < steps:
            convert(lax.rem(y - s + ny, ny))
            convert(lax.rem(y + s, ny))
        else:
            convert(lax.rem(y + s, ny))
        if s == steps - 1:
            local[2].wait()
            for d in (1, 3, 2):
                s_out[d].wait_recv()
            for k in range(X):
                hi, lo = split_hi_lo(sbuf[k])
                bhi[pl.ds(k * rows, rows), :] = hi
                blo[pl.ds(k * rows, rows), :] = lo

    for p in range(2):
        for r in range(ny):
            for k in range(X):
                tmat[p, pl.ds((r * X + k) * 4, 4), :] = vbuf[r, k, p, :, pl.ds(width, LANE)]

    part[...] = jnp.zeros_like(part)
    sl = pl.ds(0, LANE)
    v1 = pl.ds(LANE, LANE)
    v2 = pl.ds(2 * LANE, LANE)
    both = pl.ds(0, 2 * LANE)
    nt = ((1,), (1,))

    @pl.loop(0, chunks)
    def _(k):
        cols = pl.ds(pl.multiple_of(k * wide, LANE), wide)

        def three(a, b):
            return (
                dot_bf16(bhi[a, cols], bhi[b, cols], nt)
                + dot_bf16(bhi[a, cols], blo[b, cols], nt)
                + dot_bf16(blo[a, cols], bhi[b, cols], nt)
            )

        part[:, pl.ds(0, LANE)] += three(sl, v1)
        lower = three(both, v2)
        part[:, pl.ds(LANE, LANE)] += lower[:LANE]
        part[:, pl.ds(2 * LANE, LANE)] += lower[LANE:]

    piece = LANE // members

    def mine(index):
        return pl.ds(pl.multiple_of(index * piece, 8), piece)

    a_out = []
    for d in (4, 3, 5, 2, 6, 1, 7):
        copy = remote(part.at[mine(lax.rem(m + d, members))], ra.at[d], a_s.at[d], a_r.at[d], in_group(d))
        copy.start()
        a_out.append(copy)
    for copy in a_out:
        copy.wait_recv()
    total = part[mine(m), :]
    for d in range(1, members):
        total = total + ra[d]
    qsum[...] = total

    b_out = []
    for d in (4, 3, 5, 2, 6, 1, 7):
        copy = remote(qsum, rb.at[d], b_s.at[d], b_r.at[d], along_z(d))
        copy.start()
        b_out.append(copy)
    for copy in b_out:
        copy.wait_recv()
    for d in range(1, nz):
        total = total + rb[d]
    rc[mine(m), :] = total

    c_out = []
    for d in (4, 3, 5, 2, 6, 1, 7):
        copy = remote(rc.at[mine(m)], rc.at[mine(m)], c_s.at[d], c_r.at[d], in_group(d))
        copy.start()
        c_out.append(copy)
    for copy in c_out:
        copy.wait_recv()

    gram = rc[:, pl.ds(2 * LANE, LANE)]
    upper = dot_f32(rc[:, pl.ds(0, LANE)], tmat[0], nt)
    rest = rc[:, pl.ds(LANE, LANE)] - dot_f32(upper, gram, ((1,), (0,)))
    lower = dot_f32(rest, tmat[1], nt)
    for p, value in enumerate((upper, lower)):
        hi, lo = split_hi_lo(value)
        yhi[:, pl.ds(p * LANE, LANE)] = hi
        ylo[:, pl.ds(p * LANE, LANE)] = lo

    nn = ((1,), (0,))
    vectors = pl.ds(LANE, 2 * LANE)

    def block(k, d, skip):
        to = lax.rem(x + d, X)
        mine_rows = pl.ds(pl.multiple_of(to * rows, 8), rows)
        src = obuf.at[k, mine_rows, pl.ds(skip, wide - skip)]
        dst = o_hbm.at[:, pl.ds(pl.multiple_of(own_start + k * wide + skip, LANE), wide - skip)]
        return src, dst

    def ship(k, skip):
        for d in (2, 1, 3):
            src, dst = block(k, d, skip)
            remote(src, dst, o_s.at[k, d], o_r.at[k, d], along_x(d)).start()
        src, dst = block(k, 0, skip)
        pltpu.make_async_copy(src, dst, o_l.at[k]).start()

    def shipped(k, skip):
        for d in (2, 1, 3):
            src, dst = block(k, d, skip)
            remote(src, dst, o_s.at[k, d], o_r.at[k, d], along_x(d)).wait_send()
        src, dst = block(k, 0, skip)
        pltpu.make_async_copy(src, dst, o_l.at[k]).wait()

    def by_width(k, act, where_x):
        if k > 0:
            act(k, 0)
            return

        @pl.when(where_x < 2)
        def _():
            act(k, 0)

        @pl.when(where_x >= 2)
        def _():
            act(k, LANE)

    for k in range(chunks):
        cols = pl.ds(k * wide, wide)
        change = (
            dot_bf16(yhi[...], bhi[vectors, cols], nn)
            + dot_bf16(yhi[...], blo[vectors, cols], nn)
            + dot_bf16(ylo[...], bhi[vectors, cols], nn)
        )
        for q in range(X):
            obuf[k, pl.ds(q * rows, rows), :] = sbuf[q, :, cols] - change[q * rows : (q + 1) * rows]
        if k > 0:
            by_width(k - 1, ship, x)
    by_width(chunks - 1, ship, x)

    for d in (1, 3, 2):
        v_out[d].wait_send()
        t_out[d].wait_send()
        s_out[d].wait_send()
    for copy in sent + a_out + b_out + c_out:
        copy.wait_send()
    for k in range(chunks):
        by_width(k, shipped, x)
        for d in (2, 1, 3):
            source = lax.rem(x + X - d, X)

            def arrived(k, skip, d=d):
                src, dst = block(k, d, skip)
                remote(src, dst, o_s.at[k, d], o_r.at[k, d], along_x(d)).wait_recv()

            by_width(k, arrived, source)


def solution(mesh):
    ny, nz = mesh.shape["pcol"] // X, mesh.shape["prow"] // 2

    def body(slab, reflectors, factors):
        rows, entries = slab.shape
        width = -(-entries // (X * LANE)) * LANE
        chunks = 5
        wide = width // chunks
        f32, bf16 = jnp.float32, jnp.bfloat16
        vmem, dma = pltpu.VMEM, pltpu.SemaphoreType.DMA
        any_space = pl.BlockSpec(memory_space=pl.ANY)
        return pl.pallas_call(
            functools.partial(kernel, (ny, nz, rows, width, chunks)),
            out_shape=jax.ShapeDtypeStruct(slab.shape, f32),
            in_specs=[any_space] * 3,
            out_specs=any_space,
            scratch_shapes=[
                vmem((ny, X, 2, 4, width + LANE), f32),
                vmem((X, rows, width), f32),
                vmem((3 * LANE, width), bf16),
                vmem((3 * LANE, width), bf16),
                vmem((2, LANE, LANE), f32),
                vmem((LANE, 3 * LANE), f32),
                vmem((2 * X, 16, 3 * LANE), f32),
                vmem((16, 3 * LANE), f32),
                vmem((nz, 16, 3 * LANE), f32),
                vmem((LANE, 3 * LANE), f32),
                vmem((LANE, 2 * LANE), bf16),
                vmem((LANE, 2 * LANE), bf16),
                vmem((chunks, X * rows, wide), f32),
                dma((X,)), dma((X,)), dma((X,)), dma((X,)), dma((X,)), dma((X,)),
                dma((3,)),
                dma((2, ny // 2, X)), dma((2, ny // 2, X)),
                dma((2 * X,)), dma((2 * X,)), dma((nz,)), dma((nz,)), dma((2 * X,)), dma((2 * X,)),
                dma((chunks, X)), dma((chunks, X)), dma((chunks,)),
            ],
            compiler_params=pltpu.CompilerParams(
                collective_id=0, has_side_effects=True, vmem_limit_bytes=48 << 20
            ),
            name="backtransform",
        )(slab, reflectors, factors)

    in_specs = (P("pcol", "prow"), P(None, "pcol", "prow"), P(None, "pcol", None))
    return jax.shard_map(body, mesh=mesh, in_specs=in_specs, out_specs=P("pcol", "prow"), check_vma=False)
```

```python
import functools

import jax
import jax.numpy as jnp
from jax import lax
from jax.experimental import pallas as pl
from jax.experimental.pallas import tpu as pltpu
from jax.sharding import PartitionSpec as P

X = 4
MESH = pl.DeviceIdType.MESH
LANE = 128


def quarter_start(x):
    return pl.multiple_of((24 * x + (x + X - 1) // X) * LANE, LANE)


def dot_f32(left, right, dims):
    return lax.dot_general(
        left, right, (dims, ((), ())), precision=lax.Precision.HIGHEST, preferred_element_type=jnp.float32
    )


def dot_bf16(left, right, dims):
    return lax.dot_general(left, right, (dims, ((), ())), preferred_element_type=jnp.float32)


def split_hi_lo(value):
    hi = value.astype(jnp.bfloat16)
    lo = (value - hi.astype(jnp.float32)).astype(jnp.bfloat16)
    return hi, lo


def kernel(
    dims, s_hbm, v_hbm, t_hbm, o_hbm,
    vbuf, sbuf, bhi, blo, tmat, part, gram, ra, qsum, rb, rc, yhi, ylo, obuf,
    vx_s, vx_r, tx_s, tx_r, sx_s, sx_r, loc, ys, yr, a_s, a_r, b_s, b_r, c_s, c_r, o_s, o_r, o_l,
):
    ny, nz, rows, width, chunks = dims
    wide = width // chunks
    pr, pc = lax.axis_index("prow"), lax.axis_index("pcol")
    x, y, z, c = lax.rem(pc, X), pc // X, pr // 2, lax.rem(pr, 2)
    m = x * 2 + c
    members = 2 * X
    piece = LANE // members
    far = (4, 3, 5, 2, 6, 1, 7)

    def at(x_to, y_to, z_to, c_to):
        return {"prow": z_to * 2 + c_to, "pcol": y_to * X + x_to}

    def along_x(d):
        return at(lax.rem(x + d, X), y, z, c)

    def along_y(d):
        return at(x, lax.rem(y + d + ny, ny), z, c)

    def along_z(d):
        return at(x, y, lax.rem(z + d, nz), c)

    def in_group(d):
        to = lax.rem(m + d, members)
        return at(to // 2, y, z, lax.rem(to, 2))

    def remote(src, dst, send, recv, to):
        return pltpu.make_async_remote_copy(
            src_ref=src, dst_ref=dst, send_sem=send, recv_sem=recv, device_id=to, device_id_type=MESH
        )

    own_start = quarter_start(x)
    local = []
    for p in range(2):
        local.append(
            pltpu.make_async_copy(
                v_hbm.at[p, :, pl.ds(own_start, width)], vbuf.at[p, y, x, :, pl.ds(0, width)], loc.at[p]
            )
        )
        local.append(pltpu.make_async_copy(t_hbm.at[p], vbuf.at[p, y, x, :, pl.ds(width, LANE)], loc.at[2 + p]))
    local.append(pltpu.make_async_copy(s_hbm.at[:, pl.ds(own_start, width)], sbuf.at[x], loc.at[4]))
    for copy in local:
        copy.start()

    barrier = pltpu.get_barrier_semaphore()
    peers = [along_y(1), along_y(-1)] + [in_group(d) for d in range(1, members)] + [along_z(d) for d in range(1, nz)]
    for to in peers:
        pl.semaphore_signal(barrier, inc=1, device_id=to, device_id_type=MESH)
    pl.semaphore_wait(barrier, len(peers))

    v_out, t_out, s_out = {}, {}, {}
    for p in range(2):
        for d in (1, 3, 2):
            start = quarter_start(lax.rem(x + d, X))
            v_out[p, d] = remote(
                v_hbm.at[p, :, pl.ds(start, width)], vbuf.at[p, y, x, :, pl.ds(0, width)],
                vx_s.at[p, d], vx_r.at[p, d], along_x(d),
            )
            t_out[p, d] = remote(
                t_hbm.at[p], vbuf.at[p, y, x, :, pl.ds(width, LANE)], tx_s.at[p, d], tx_r.at[p, d], along_x(d)
            )
            v_out[p, d].start()
            t_out[p, d].start()
    for d in (1, 3, 2):
        start = quarter_start(lax.rem(x + d, X))
        s_out[d] = remote(s_hbm.at[:, pl.ds(start, width)], sbuf.at[x], sx_s.at[d], sx_r.at[d], along_x(d))
        s_out[d].start()

    def convert(p, row):
        keep = jnp.where(x < 2, 1.0, 0.0)
        base = pl.multiple_of(X * rows + p * LANE + row * 16, 16)
        value = jnp.concatenate([vbuf[p, row, k, :, pl.ds(0, width)] for k in range(X)], axis=0)
        value = jnp.concatenate([value[:, :LANE] * keep, value[:, LANE:]], axis=1)
        hi, lo = split_hi_lo(value)
        bhi[pl.ds(base, 16), :] = hi
        blo[pl.ds(base, 16), :] = lo

    steps = ny // 2
    orders = (((0, 1, 3, 2),) * 3 + ((0, 1),), ((0, 3, 1, 2), (3, 0, 2, 1), (3, 2, 0, 1), (3, 2)))
    sent = []

    def hop(p, s, j, way):
        sign = 1 if way == 0 else -1
        row = lax.rem(y - sign * s + ny, ny)
        slot = vbuf.at[p, row, lax.rem(x + j, X)]
        return remote(slot, slot, ys.at[p, way, s, j], yr.at[p, way, s, j], along_y(sign))

    def came(p, s, j, way):
        sign = 1 if way == 0 else -1
        row = lax.rem(y - sign * (s + 1) + ny, ny)
        slot = vbuf.at[p, row, lax.rem(x + j, X)]
        remote(slot, slot, ys.at[p, way, s, j], yr.at[p, way, s, j], along_y(sign)).wait_recv()

    def ring_step(p, s, pick=None):
        ready = set()
        for i in range(X):
            for way in range(2):
                if s == 0:
                    j = orders[way][0][i]
                    if pick is not None and j not in pick:
                        continue
                    if j not in ready:
                        ready.add(j)
                        if j == 0:
                            local[2 * p].wait()
                            local[2 * p + 1].wait()
                        else:
                            v_out[p, X - j].wait_recv()
                            t_out[p, X - j].wait_recv()
                    sends = True
                else:
                    full = orders[way][min(s, 2)] if s < steps else orders[way][3]
                    if i >= len(full):
                        continue
                    j = full[i]
                    came(p, s - 1, j, way)
                    sends = s < steps and j in orders[way][s]
                if sends:
                    copy = hop(p, s, j, way)
                    copy.start()
                    sent.append(copy)

    def convert_step(p, s):
        convert(p, lax.rem(y + s, ny))
        if 0 < s < steps:
            convert(p, lax.rem(y - s + ny, ny))

    nt, nn = ((1,), (1,)), ((1,), (0,))

    def mine(index):
        return pl.ds(pl.multiple_of(index * piece, 8), piece)

    def products(targets, left, right):
        for ref, _ in targets:
            ref[...] = jnp.zeros_like(ref)

        @pl.loop(0, chunks)
        def _(k):
            cols = pl.ds(pl.multiple_of(k * wide, LANE), wide)
            value = (
                dot_bf16(bhi[left, cols], bhi[right, cols], nt)
                + dot_bf16(bhi[left, cols], blo[right, cols], nt)
                + dot_bf16(blo[left, cols], bhi[right, cols], nt)
            )
            for ref, lo in targets:
                ref[...] += value[lo : lo + LANE]

    started = []

    def scatter_start(p):
        for d in far:
            copy = remote(
                part.at[p, mine(lax.rem(m + d, members))], ra.at[p, d], a_s.at[p, d], a_r.at[p, d], in_group(d)
            )
            copy.start()
            started.append(copy)

    def column_start(p):
        total = part[p, mine(m), :]
        for d in range(1, members):
            remote(part.at[p, mine(m)], ra.at[p, d], a_s.at[p, d], a_r.at[p, d], in_group(d)).wait_recv()
        for d in range(1, members):
            total = total + ra[p, d]
        qsum[p] = total
        for d in far:
            copy = remote(qsum.at[p], rb.at[p, d], b_s.at[p, d], b_r.at[p, d], along_z(d))
            copy.start()
            started.append(copy)

    def spread_start(p):
        total = qsum[p]
        for d in range(1, nz):
            remote(qsum.at[p], rb.at[p, d], b_s.at[p, d], b_r.at[p, d], along_z(d)).wait_recv()
        for d in range(1, nz):
            total = total + rb[p, d]
        rc[p, mine(m), :] = total
        for d in far:
            copy = remote(rc.at[p, mine(m)], rc.at[p, mine(m)], c_s.at[p, d], c_r.at[p, d], in_group(d))
            copy.start()
            started.append(copy)

    def spread_done(p):
        for d in range(1, members):
            theirs = rc.at[p, mine(lax.rem(m + members - d, members))]
            remote(theirs, theirs, c_s.at[p, d], c_r.at[p, d], in_group(d)).wait_recv()

    def scale(p, value):
        hi, lo = split_hi_lo(value)
        yhi[p] = hi
        ylo[p] = lo

    def change(p, cols):
        vectors = pl.ds(X * rows + p * LANE, LANE)
        return (
            dot_bf16(yhi[p], bhi[vectors, cols], nn)
            + dot_bf16(yhi[p], blo[vectors, cols], nn)
            + dot_bf16(ylo[p], bhi[vectors, cols], nn)
        )

    def triangle(p):
        for r in range(ny):
            for k in range(X):
                tmat[p, pl.ds((r * X + k) * 4, 4), :] = vbuf[p, r, k, :, pl.ds(width, LANE)]

    ring_step(0, 0, (0,))
    ring_step(1, 0, (0,))
    ring_step(0, 0, (1, 2, 3))
    convert_step(0, 0)
    ring_step(0, 1)
    convert_step(0, 1)
    ring_step(0, 2)
    ring_step(1, 0, (1, 2, 3))
    convert_step(0, 2)
    ring_step(0, 3)
    convert_step(0, 3)
    convert_step(1, 0)
    ring_step(0, 4)
    ring_step(1, 1)
    convert_step(0, 4)
    triangle(0)

    local[4].wait()
    for d in (1, 3, 2):
        s_out[d].wait_recv()
    for k in range(X):
        hi, lo = split_hi_lo(sbuf[k])
        bhi[pl.ds(k * rows, rows), :] = hi
        blo[pl.ds(k * rows, rows), :] = lo
    products([(part.at[0], 0)], pl.ds(0, LANE), pl.ds(LANE, LANE))
    scatter_start(0)
    convert_step(1, 1)
    ring_step(1, 2)
    column_start(0)
    convert_step(1, 2)
    ring_step(1, 3)
    spread_start(0)
    convert_step(1, 3)
    ring_step(1, 4)
    convert_step(1, 4)
    triangle(1)
    products([(part.at[1], 0), (gram, LANE)], pl.ds(0, 2 * LANE), pl.ds(2 * LANE, LANE))
    spread_done(0)
    upper = dot_f32(rc[0], tmat[0], nt)
    part[1] = part[1] - dot_f32(upper, gram[...], nn)
    scatter_start(1)
    scale(0, upper)

    def first_change(k):
        cols = pl.ds(k * wide, wide)
        value = change(0, cols)
        for q in range(X):
            obuf[k, pl.ds(q * rows, rows), :] = sbuf[q, :, cols] - value[q * rows : (q + 1) * rows]

    first_change(0)
    first_change(1)
    column_start(1)
    first_change(2)
    first_change(3)
    spread_start(1)
    first_change(4)
    spread_done(1)
    scale(1, dot_f32(rc[1], tmat[1], nt))

    def block(k, d, skip):
        to = lax.rem(x + d, X)
        mine_rows = pl.ds(pl.multiple_of(to * rows, 8), rows)
        src = obuf.at[k, mine_rows, pl.ds(skip, wide - skip)]
        dst = o_hbm.at[:, pl.ds(pl.multiple_of(own_start + k * wide + skip, LANE), wide - skip)]
        return src, dst

    def ship(k, skip):
        for d in (2, 1, 3):
            src, dst = block(k, d, skip)
            remote(src, dst, o_s.at[k, d], o_r.at[k, d], along_x(d)).start()
        src, dst = block(k, 0, skip)
        pltpu.make_async_copy(src, dst, o_l.at[k]).start()

    def shipped(k, skip):
        for d in (2, 1, 3):
            src, dst = block(k, d, skip)
            remote(src, dst, o_s.at[k, d], o_r.at[k, d], along_x(d)).wait_send()
        src, dst = block(k, 0, skip)
        pltpu.make_async_copy(src, dst, o_l.at[k]).wait()

    def by_width(k, act, where_x):
        if k > 0:
            act(k, 0)
            return

        @pl.when(where_x < 2)
        def _():
            act(k, 0)

        @pl.when(where_x >= 2)
        def _():
            act(k, LANE)

    for k in range(chunks):
        cols = pl.ds(k * wide, wide)
        obuf[k] = obuf[k] - change(1, cols)
        if k > 0:
            by_width(k - 1, ship, x)
    by_width(chunks - 1, ship, x)

    for d in (1, 3, 2):
        for p in range(2):
            v_out[p, d].wait_send()
            t_out[p, d].wait_send()
        s_out[d].wait_send()
    for copy in sent + started:
        copy.wait_send()
    for k in range(chunks):
        by_width(k, shipped, x)
        for d in (2, 1, 3):
            source = lax.rem(x + X - d, X)

            def arrived(k, skip, d=d):
                src, dst = block(k, d, skip)
                remote(src, dst, o_s.at[k, d], o_r.at[k, d], along_x(d)).wait_recv()

            by_width(k, arrived, source)


def solution(mesh):
    ny, nz = mesh.shape["pcol"] // X, mesh.shape["prow"] // 2

    def body(slab, reflectors, factors):
        rows, entries = slab.shape
        width = -(-entries // (X * LANE)) * LANE
        chunks = 5
        wide = width // chunks
        f32, bf16 = jnp.float32, jnp.bfloat16
        vmem, dma = pltpu.VMEM, pltpu.SemaphoreType.DMA
        any_space = pl.BlockSpec(memory_space=pl.ANY)
        return pl.pallas_call(
            functools.partial(kernel, (ny, nz, rows, width, chunks)),
            out_shape=jax.ShapeDtypeStruct(slab.shape, f32),
            in_specs=[any_space] * 3,
            out_specs=any_space,
            scratch_shapes=[
                vmem((2, ny, X, 4, width + LANE), f32),
                vmem((X, rows, width), f32),
                vmem((3 * LANE, width), bf16),
                vmem((3 * LANE, width), bf16),
                vmem((2, LANE, LANE), f32),
                vmem((2, LANE, LANE), f32),
                vmem((LANE, LANE), f32),
                vmem((2, 2 * X, 16, LANE), f32),
                vmem((2, 16, LANE), f32),
                vmem((2, nz, 16, LANE), f32),
                vmem((2, LANE, LANE), f32),
                vmem((2, LANE, LANE), bf16),
                vmem((2, LANE, LANE), bf16),
                vmem((chunks, X * rows, wide), f32),
                dma((2, X)), dma((2, X)), dma((2, X)), dma((2, X)), dma((X,)), dma((X,)),
                dma((5,)),
                dma((2, 2, ny // 2, X)), dma((2, 2, ny // 2, X)),
                dma((2, 2 * X)), dma((2, 2 * X)), dma((2, nz)), dma((2, nz)), dma((2, 2 * X)), dma((2, 2 * X)),
                dma((chunks, X)), dma((chunks, X)), dma((chunks,)),
            ],
            compiler_params=pltpu.CompilerParams(
                collective_id=0, has_side_effects=True, vmem_limit_bytes=40 << 20
            ),
            name="backtransform",
        )(*(pltpu.with_memory_space_constraint(a, pltpu.HBM) for a in (slab, reflectors, factors)))

    in_specs = (P("pcol", "prow"), P(None, "pcol", "prow"), P(None, "pcol", None))
    return jax.shard_map(body, mesh=mesh, in_specs=in_specs, out_specs=P("pcol", "prow"), check_vma=False)
```

```python
import functools

import jax
import jax.numpy as jnp
from jax import lax
from jax.experimental import pallas as pl
from jax.experimental.pallas import tpu as pltpu
from jax.sharding import PartitionSpec as P

X = 4
MESH = pl.DeviceIdType.MESH
LANE = 128
LENT = 2


def quarter_start(x):
    return pl.multiple_of((24 * x + (x + X - 1) // X) * LANE, LANE)


def dot_f32(left, right, dims):
    return lax.dot_general(
        left, right, (dims, ((), ())), precision=lax.Precision.HIGHEST, preferred_element_type=jnp.float32
    )


def dot_bf16(left, right, dims):
    return lax.dot_general(left, right, (dims, ((), ())), preferred_element_type=jnp.float32)


def split_hi_lo(value):
    hi = value.astype(jnp.bfloat16)
    lo = (value - hi.astype(jnp.float32)).astype(jnp.bfloat16)
    return hi, lo


def kernel(
    dims, s_hbm, v_hbm, t_hbm, o_hbm,
    vbuf, sbuf, bhi, blo, tmat, part, gram, ra, qsum, rb, rc, yhi, ylo, obuf, pbuf, phi, plo, sbase, fbuf,
    vx_s, vx_r, tx_s, tx_r, sx_s, sx_r, loc, ys, yr, a_s, a_r, b_s, b_r, c_s, c_r, o_s, o_r, o_l, p_s, p_r, q_s, q_r, f_l,
):
    ny, nz, rows, width, chunks = dims
    wide = width // chunks
    pr, pc = lax.axis_index("prow"), lax.axis_index("pcol")
    x, y, z, c = lax.rem(pc, X), pc // X, pr // 2, lax.rem(pr, 2)
    m = x * 2 + c
    members = 2 * X
    piece = LANE // members
    far = (4, 3, 5, 2, 6, 1, 7)

    def at(x_to, y_to, z_to, c_to):
        return {"prow": z_to * 2 + c_to, "pcol": y_to * X + x_to}

    def along_x(d):
        return at(lax.rem(x + d, X), y, z, c)

    def along_y(d):
        return at(x, lax.rem(y + d + ny, ny), z, c)

    def along_z(d):
        return at(x, y, lax.rem(z + d, nz), c)

    def in_group(d):
        to = lax.rem(m + d, members)
        return at(to // 2, y, z, lax.rem(to, 2))

    def remote(src, dst, send, recv, to):
        return pltpu.make_async_remote_copy(
            src_ref=src, dst_ref=dst, send_sem=send, recv_sem=recv, device_id=to, device_id_type=MESH
        )

    own_start = quarter_start(x)
    local = []
    for p in range(2):
        local.append(
            pltpu.make_async_copy(
                v_hbm.at[p, :, pl.ds(own_start, width)], vbuf.at[p, y, x, :, pl.ds(0, width)], loc.at[p]
            )
        )
        local.append(pltpu.make_async_copy(t_hbm.at[p], vbuf.at[p, y, x, :, pl.ds(width, LANE)], loc.at[2 + p]))
    local.append(pltpu.make_async_copy(s_hbm.at[:, pl.ds(own_start, width)], sbuf.at[x], loc.at[4]))
    for copy in local:
        copy.start()

    barrier = pltpu.get_barrier_semaphore()
    peers = [along_y(1), along_y(-1)] + [in_group(d) for d in range(1, members)] + [along_z(d) for d in range(1, nz)]
    for to in peers:
        pl.semaphore_signal(barrier, inc=1, device_id=to, device_id_type=MESH)
    pl.semaphore_wait(barrier, len(peers))

    v_out, t_out, s_out = {}, {}, {}
    for p in range(2):
        for d in (1, 3, 2):
            start = quarter_start(lax.rem(x + d, X))
            v_out[p, d] = remote(
                v_hbm.at[p, :, pl.ds(start, width)], vbuf.at[p, y, x, :, pl.ds(0, width)],
                vx_s.at[p, d], vx_r.at[p, d], along_x(d),
            )
            t_out[p, d] = remote(
                t_hbm.at[p], vbuf.at[p, y, x, :, pl.ds(width, LANE)], tx_s.at[p, d], tx_r.at[p, d], along_x(d)
            )
            v_out[p, d].start()
            t_out[p, d].start()
    for d in (1, 3, 2):
        start = quarter_start(lax.rem(x + d, X))
        s_out[d] = remote(s_hbm.at[:, pl.ds(start, width)], sbuf.at[x], sx_s.at[d], sx_r.at[d], along_x(d))
        s_out[d].start()

    def convert(p, row):
        keep = jnp.where(x < 2, 1.0, 0.0)
        base = pl.multiple_of(X * rows + p * LANE + row * 16, 16)
        value = jnp.concatenate([vbuf[p, row, k, :, pl.ds(0, width)] for k in range(X)], axis=0)
        value = jnp.concatenate([value[:, :LANE] * keep, value[:, LANE:]], axis=1)
        hi, lo = split_hi_lo(value)
        bhi[pl.ds(base, 16), :] = hi
        blo[pl.ds(base, 16), :] = lo

    steps = ny // 2
    orders = (((0, 1, 3, 2),) * 3 + ((0, 1),), ((0, 3, 1, 2), (3, 0, 2, 1), (3, 2, 0, 1), (3, 2)))
    sent = []

    def hop(p, s, j, way):
        sign = 1 if way == 0 else -1
        row = lax.rem(y - sign * s + ny, ny)
        slot = vbuf.at[p, row, lax.rem(x + j, X)]
        return remote(slot, slot, ys.at[p, way, s, j], yr.at[p, way, s, j], along_y(sign))

    def came(p, s, j, way):
        sign = 1 if way == 0 else -1
        row = lax.rem(y - sign * (s + 1) + ny, ny)
        slot = vbuf.at[p, row, lax.rem(x + j, X)]
        remote(slot, slot, ys.at[p, way, s, j], yr.at[p, way, s, j], along_y(sign)).wait_recv()

    def ring_step(p, s, pick=None):
        ready = set()
        for i in range(X):
            for way in range(2):
                if s == 0:
                    j = orders[way][0][i]
                    if pick is not None and j not in pick:
                        continue
                    if j not in ready:
                        ready.add(j)
                        if j == 0:
                            local[2 * p].wait()
                            local[2 * p + 1].wait()
                        else:
                            v_out[p, X - j].wait_recv()
                            t_out[p, X - j].wait_recv()
                    sends = True
                else:
                    full = orders[way][min(s, 2)] if s < steps else orders[way][3]
                    if i >= len(full):
                        continue
                    j = full[i]
                    came(p, s - 1, j, way)
                    sends = s < steps and j in orders[way][s]
                if sends:
                    copy = hop(p, s, j, way)
                    copy.start()
                    sent.append(copy)

    def convert_step(p, s):
        convert(p, lax.rem(y + s, ny))
        if 0 < s < steps:
            convert(p, lax.rem(y - s + ny, ny))

    nt, nn = ((1,), (1,)), ((1,), (0,))

    def mine(index):
        return pl.ds(pl.multiple_of(index * piece, 8), piece)

    def products(targets, left, right):
        for ref, _ in targets:
            ref[...] = jnp.zeros_like(ref)

        @pl.loop(0, chunks)
        def _(k):
            cols = pl.ds(pl.multiple_of(k * wide, LANE), wide)
            value = (
                dot_bf16(bhi[left, cols], bhi[right, cols], nt)
                + dot_bf16(bhi[left, cols], blo[right, cols], nt)
                + dot_bf16(blo[left, cols], bhi[right, cols], nt)
            )
            for ref, lo in targets:
                ref[...] += value[lo : lo + LANE]

    started = []

    def scatter_start(p):
        for d in far:
            copy = remote(
                part.at[p, mine(lax.rem(m + d, members))], ra.at[p, d], a_s.at[p, d], a_r.at[p, d], in_group(d)
            )
            copy.start()
            started.append(copy)

    def column_start(p):
        total = part[p, mine(m), :]
        for d in range(1, members):
            remote(part.at[p, mine(m)], ra.at[p, d], a_s.at[p, d], a_r.at[p, d], in_group(d)).wait_recv()
        for d in range(1, members):
            total = total + ra[p, d]
        qsum[p] = total
        for d in far:
            copy = remote(qsum.at[p], rb.at[p, d], b_s.at[p, d], b_r.at[p, d], along_z(d))
            copy.start()
            started.append(copy)

    def spread_start(p):
        total = qsum[p]
        for d in range(1, nz):
            remote(qsum.at[p], rb.at[p, d], b_s.at[p, d], b_r.at[p, d], along_z(d)).wait_recv()
        for d in range(1, nz):
            total = total + rb[p, d]
        rc[p, mine(m), :] = total
        for d in far:
            copy = remote(rc.at[p, mine(m)], rc.at[p, mine(m)], c_s.at[p, d], c_r.at[p, d], in_group(d))
            copy.start()
            started.append(copy)

    def spread_done(p):
        for d in range(1, members):
            theirs = rc.at[p, mine(lax.rem(m + members - d, members))]
            remote(theirs, theirs, c_s.at[p, d], c_r.at[p, d], in_group(d)).wait_recv()

    def scale(p, value):
        hi, lo = split_hi_lo(value)
        yhi[p] = hi
        ylo[p] = lo

    def change(p, cols):
        vectors = pl.ds(X * rows + p * LANE, LANE)
        return (
            dot_bf16(yhi[p], bhi[vectors, cols], nn)
            + dot_bf16(yhi[p], blo[vectors, cols], nn)
            + dot_bf16(ylo[p], bhi[vectors, cols], nn)
        )

    def triangle(p):
        for r in range(ny):
            for k in range(X):
                tmat[p, pl.ds((r * X + k) * 4, 4), :] = vbuf[p, r, k, :, pl.ds(width, LANE)]

    items = (0, 1, -1, 2, -2, 3, -3, 4)
    sides = (1, 3)
    kept = chunks - LENT
    lent_at, lent = kept * wide, LENT * wide

    def lend(*which):
        for q in which:
            row = lax.rem(y + items[q] + ny, ny)
            for i, d in enumerate(sides):
                copy = remote(
                    vbuf.at[1, row, :, :, pl.ds(lent_at, lent)], pbuf.at[i, row], p_s.at[i, q], p_r.at[i, q], along_x(d)
                )
                copy.start()
                started.append(copy)

    def borrow(*which):
        for q in which:
            row = lax.rem(y + items[q] + ny, ny)
            for i, d in enumerate(sides):
                remote(
                    vbuf.at[1, row, :, :, pl.ds(lent_at, lent)], pbuf.at[i, row], p_s.at[i, q], p_r.at[i, q], along_x(d)
                ).wait_recv()
                base = pl.multiple_of(row * 16, 16)
                hi, lo = split_hi_lo(jnp.concatenate([pbuf[i, row, k] for k in range(X)], axis=0))
                phi[i, pl.ds(base, 16), :] = hi
                plo[i, pl.ds(base, 16), :] = lo

    def base_copy(k, i):
        theirs = pl.ds(pl.multiple_of(lax.rem(x + sides[i], X) * rows, 8), rows)
        return remote(
            obuf.at[k, theirs], sbase.at[i, k - kept], q_s.at[i, k - kept], q_r.at[i, k - kept], along_x(sides[i])
        )

    ring_step(0, 0, (0,))
    ring_step(1, 0, (0,))
    ring_step(0, 0, (1, 2, 3))
    convert_step(0, 0)
    ring_step(0, 1)
    convert_step(0, 1)
    ring_step(0, 2)
    ring_step(1, 0, (1, 2, 3))
    convert_step(0, 2)
    ring_step(0, 3)
    convert_step(0, 3)
    convert_step(1, 0)
    ring_step(0, 4)
    ring_step(1, 1)
    convert_step(0, 4)
    triangle(0)

    local[4].wait()
    for d in (1, 3, 2):
        s_out[d].wait_recv()
    for k in range(X):
        hi, lo = split_hi_lo(sbuf[k])
        bhi[pl.ds(k * rows, rows), :] = hi
        blo[pl.ds(k * rows, rows), :] = lo
    products([(part.at[0], 0)], pl.ds(0, LANE), pl.ds(LANE, LANE))
    scatter_start(0)
    convert_step(1, 1)
    lend(0, 1, 2)
    ring_step(1, 2)
    column_start(0)
    convert_step(1, 2)
    lend(3, 4)
    ring_step(1, 3)
    spread_start(0)
    convert_step(1, 3)
    lend(5, 6)
    ring_step(1, 4)
    convert_step(1, 4)
    triangle(1)
    products([(part.at[1], 0), (gram, LANE)], pl.ds(0, 2 * LANE), pl.ds(2 * LANE, LANE))
    spread_done(0)
    upper = dot_f32(rc[0], tmat[0], nt)
    part[1] = part[1] - dot_f32(upper, gram[...], nn)
    scatter_start(1)
    scale(0, upper)

    def first_change(k):
        cols = pl.ds(k * wide, wide)
        value = change(0, cols)
        for q in range(X):
            obuf[k, pl.ds(q * rows, rows), :] = sbuf[q, :, cols] - value[q * rows : (q + 1) * rows]

    lend(7)
    for k in range(kept, chunks):
        first_change(k)
        for i in range(2):
            copy = base_copy(k, i)
            copy.start()
    first_change(0)
    column_start(1)
    for k in range(1, kept):
        first_change(k)
    borrow(0, 1, 2, 3, 4)
    spread_start(1)
    borrow(5, 6, 7)
    spread_done(1)
    scale(1, dot_f32(rc[1], tmat[1], nt))

    def block(k, d, skip):
        to = lax.rem(x + d, X)
        mine_rows = pl.ds(pl.multiple_of(to * rows, 8), rows)
        src = obuf.at[k, mine_rows, pl.ds(skip, wide - skip)]
        dst = o_hbm.at[:, pl.ds(pl.multiple_of(own_start + k * wide + skip, LANE), wide - skip)]
        return src, dst

    def outward(k):
        return (2, 1, 3) if k < kept else (2,)

    def ship(k, skip):
        for d in outward(k):
            src, dst = block(k, d, skip)
            remote(src, dst, o_s.at[k, d], o_r.at[k, d], along_x(d)).start()
        src, dst = block(k, 0, skip)
        pltpu.make_async_copy(src, dst, o_l.at[k]).start()

    def shipped(k, skip):
        for d in outward(k):
            src, dst = block(k, d, skip)
            remote(src, dst, o_s.at[k, d], o_r.at[k, d], along_x(d)).wait_send()
        src, dst = block(k, 0, skip)
        pltpu.make_async_copy(src, dst, o_l.at[k]).wait()

    def by_width(k, act, where_x):
        if k > 0:
            act(k, 0)
            return

        @pl.when(where_x < 2)
        def _():
            act(k, 0)

        @pl.when(where_x >= 2)
        def _():
            act(k, LANE)

    for k in range(chunks):
        cols = pl.ds(k * wide, wide)
        if k >= kept:
            for i in range(2):
                base_copy(k, i).wait_send()
        obuf[k] = obuf[k] - change(1, cols)
        if k > 0:
            by_width(k - 1, ship, x)
    by_width(chunks - 1, ship, x)

    own_rows = pl.ds(pl.multiple_of(x * rows, 16), rows)
    finished = []
    for i in range(2):
        source = lax.rem(x + X - sides[i], X)
        value = (
            dot_bf16(yhi[1, own_rows], phi[i], nn)
            + dot_bf16(yhi[1, own_rows], plo[i], nn)
            + dot_bf16(ylo[1, own_rows], phi[i], nn)
        )
        for k in range(kept, chunks):
            base_copy(k, i).wait_recv()
            part_of = pl.ds((k - kept) * wide, wide)
            fbuf[i, :, part_of] = sbase[i, k - kept] - value[:, (k - kept) * wide : (k - kept + 1) * wide]
        copy = pltpu.make_async_copy(
            fbuf.at[i],
            o_hbm.at[:, pl.ds(pl.multiple_of(quarter_start(source) + lent_at, LANE), lent)],
            f_l.at[i],
        )
        copy.start()
        finished.append(copy)

    for d in (1, 3, 2):
        for p in range(2):
            v_out[p, d].wait_send()
            t_out[p, d].wait_send()
        s_out[d].wait_send()
    for copy in sent + started:
        copy.wait_send()
    for copy in finished:
        copy.wait()
    for k in range(chunks):
        by_width(k, shipped, x)
        for d in outward(k):
            source = lax.rem(x + X - d, X)

            def arrived(k, skip, d=d):
                src, dst = block(k, d, skip)
                remote(src, dst, o_s.at[k, d], o_r.at[k, d], along_x(d)).wait_recv()

            by_width(k, arrived, source)


def solution(mesh):
    ny, nz = mesh.shape["pcol"] // X, mesh.shape["prow"] // 2

    def body(slab, reflectors, factors):
        rows, entries = slab.shape
        width = -(-entries // (X * LANE)) * LANE
        chunks = 5
        wide = width // chunks
        f32, bf16 = jnp.float32, jnp.bfloat16
        vmem, dma = pltpu.VMEM, pltpu.SemaphoreType.DMA
        any_space = pl.BlockSpec(memory_space=pl.ANY)
        return pl.pallas_call(
            functools.partial(kernel, (ny, nz, rows, width, chunks)),
            out_shape=jax.ShapeDtypeStruct(slab.shape, f32),
            in_specs=[any_space] * 3,
            out_specs=any_space,
            scratch_shapes=[
                vmem((2, ny, X, 4, width + LANE), f32),
                vmem((X, rows, width), f32),
                vmem((3 * LANE, width), bf16),
                vmem((3 * LANE, width), bf16),
                vmem((2, LANE, LANE), f32),
                vmem((2, LANE, LANE), f32),
                vmem((LANE, LANE), f32),
                vmem((2, 2 * X, 16, LANE), f32),
                vmem((2, 16, LANE), f32),
                vmem((2, nz, 16, LANE), f32),
                vmem((2, LANE, LANE), f32),
                vmem((2, LANE, LANE), bf16),
                vmem((2, LANE, LANE), bf16),
                vmem((chunks, X * rows, wide), f32),
                vmem((2, ny, X, 4, LENT * wide), f32),
                vmem((2, LANE, LENT * wide), bf16),
                vmem((2, LANE, LENT * wide), bf16),
                vmem((2, LENT, rows, wide), f32),
                vmem((2, rows, LENT * wide), f32),
                dma((2, X)), dma((2, X)), dma((2, X)), dma((2, X)), dma((X,)), dma((X,)),
                dma((5,)),
                dma((2, 2, ny // 2, X)), dma((2, 2, ny // 2, X)),
                dma((2, 2 * X)), dma((2, 2 * X)), dma((2, nz)), dma((2, nz)), dma((2, 2 * X)), dma((2, 2 * X)),
                dma((chunks, X)), dma((chunks, X)), dma((chunks,)),
                dma((2, ny)), dma((2, ny)), dma((2, LENT)), dma((2, LENT)), dma((2,)),
            ],
            compiler_params=pltpu.CompilerParams(
                collective_id=0, has_side_effects=True, vmem_limit_bytes=40 << 20
            ),
            name="backtransform",
        )(*(pltpu.with_memory_space_constraint(a, pltpu.HBM) for a in (slab, reflectors, factors)))

    in_specs = (P("pcol", "prow"), P(None, "pcol", "prow"), P(None, "pcol", None))
    return jax.shard_map(body, mesh=mesh, in_specs=in_specs, out_specs=P("pcol", "prow"), check_vma=False)
```

```python
import functools

import jax
import jax.numpy as jnp
from jax import lax
from jax.experimental import pallas as pl
from jax.experimental.pallas import tpu as pltpu
from jax.sharding import PartitionSpec as P

X = 4
MESH = pl.DeviceIdType.MESH
LANE = 128
LENT = 2
RING = 2


def quarter_start(x):
    return pl.multiple_of((24 * x + (x + X - 1) // X) * LANE, LANE)


def dot_f32(left, right, dims):
    return lax.dot_general(
        left, right, (dims, ((), ())), precision=lax.Precision.HIGHEST, preferred_element_type=jnp.float32
    )


def dot_bf16(left, right, dims):
    return lax.dot_general(left, right, (dims, ((), ())), preferred_element_type=jnp.float32)


def split_hi_lo(value):
    hi = value.astype(jnp.bfloat16)
    lo = (value - hi.astype(jnp.float32)).astype(jnp.bfloat16)
    return hi, lo


def kernel(
    dims, s_hbm, v_hbm, t_hbm, o_hbm,
    vbuf, sbuf, bhi, blo, tmat, part, gram, ra, qsum, rb, rc, yhi, ylo, obuf, pbuf, phi, plo, sbase, fbuf, vext, ehi, elo, ebase, ebuf,
    vx_s, vx_r, tx_s, tx_r, sx_s, sx_r, loc, ys, yr, a_s, a_r, b_s, b_r, c_s, c_r, o_s, o_r, o_l, p_s, p_r, q_s, q_r, f_l, ex_s, ex_r, eb_s, eb_r,
):
    ny, nz, rows, width, chunks = dims
    wide = width // chunks
    pr, pc = lax.axis_index("prow"), lax.axis_index("pcol")
    x, y, z, c = lax.rem(pc, X), pc // X, pr // 2, lax.rem(pr, 2)
    m = x * 2 + c
    members = 2 * X
    piece = LANE // members
    far = (4, 3, 5, 2, 6, 1, 7)

    def at(x_to, y_to, z_to, c_to):
        return {"prow": z_to * 2 + c_to, "pcol": y_to * X + x_to}

    def along_x(d):
        return at(lax.rem(x + d, X), y, z, c)

    def along_y(d):
        return at(x, lax.rem(y + d + ny, ny), z, c)

    def along_z(d):
        return at(x, y, lax.rem(z + d, nz), c)

    def in_group(d):
        to = lax.rem(m + d, members)
        return at(to // 2, y, z, lax.rem(to, 2))

    def remote(src, dst, send, recv, to):
        return pltpu.make_async_remote_copy(
            src_ref=src, dst_ref=dst, send_sem=send, recv_sem=recv, device_id=to, device_id_type=MESH
        )

    own_start = quarter_start(x)
    local = []
    for p in range(2):
        local.append(
            pltpu.make_async_copy(
                v_hbm.at[p, :, pl.ds(own_start, width)], vbuf.at[p, y, x, :, pl.ds(0, width)], loc.at[p]
            )
        )
        local.append(pltpu.make_async_copy(t_hbm.at[p], vbuf.at[p, y, x, :, pl.ds(width, LANE)], loc.at[2 + p]))
    local.append(pltpu.make_async_copy(s_hbm.at[:, pl.ds(own_start, width)], sbuf.at[x], loc.at[4]))
    ext, ext_at = RING * wide, (chunks - RING) * wide

    def opposite(x_of):
        start = quarter_start(lax.rem(x_of + X // 2, X)) + ext_at
        return v_hbm.at[1, :, pl.ds(pl.multiple_of(start, LANE), ext)]

    local.append(pltpu.make_async_copy(opposite(x), vext.at[y, x], loc.at[5]))
    for copy in local:
        copy.start()

    barrier = pltpu.get_barrier_semaphore()
    peers = [along_y(1), along_y(-1)] + [in_group(d) for d in range(1, members)] + [along_z(d) for d in range(1, nz)]
    for to in peers:
        pl.semaphore_signal(barrier, inc=1, device_id=to, device_id_type=MESH)
    pl.semaphore_wait(barrier, len(peers))

    v_out, t_out, s_out = {}, {}, {}
    for p in range(2):
        for d in (1, 3, 2):
            start = quarter_start(lax.rem(x + d, X))
            v_out[p, d] = remote(
                v_hbm.at[p, :, pl.ds(start, width)], vbuf.at[p, y, x, :, pl.ds(0, width)],
                vx_s.at[p, d], vx_r.at[p, d], along_x(d),
            )
            t_out[p, d] = remote(
                t_hbm.at[p], vbuf.at[p, y, x, :, pl.ds(width, LANE)], tx_s.at[p, d], tx_r.at[p, d], along_x(d)
            )
            v_out[p, d].start()
            t_out[p, d].start()
    for d in (1, 3, 2):
        start = quarter_start(lax.rem(x + d, X))
        s_out[d] = remote(s_hbm.at[:, pl.ds(start, width)], sbuf.at[x], sx_s.at[d], sx_r.at[d], along_x(d))
        s_out[d].start()

    def convert(p, row):
        keep = jnp.where(x < 2, 1.0, 0.0)
        base = pl.multiple_of(X * rows + p * LANE + row * 16, 16)
        value = jnp.concatenate([vbuf[p, row, k, :, pl.ds(0, width)] for k in range(X)], axis=0)
        value = jnp.concatenate([value[:, :LANE] * keep, value[:, LANE:]], axis=1)
        hi, lo = split_hi_lo(value)
        bhi[pl.ds(base, 16), :] = hi
        blo[pl.ds(base, 16), :] = lo

    steps = ny // 2
    orders = (((0, 1, 3, 2),) * 3 + ((0, 1),), ((0, 3, 1, 2), (3, 0, 2, 1), (3, 2, 0, 1), (3, 2)))
    sent = []

    def slot_of(p, row, j):
        from_x = lax.rem(x + j, X)
        return vext.at[row, from_x] if p == 2 else vbuf.at[p, row, from_x]

    def hop(p, s, j, way):
        sign = 1 if way == 0 else -1
        slot = slot_of(p, lax.rem(y - sign * s + ny, ny), j)
        return remote(slot, slot, ys.at[p, way, s, j], yr.at[p, way, s, j], along_y(sign))

    def came(p, s, j, way):
        sign = 1 if way == 0 else -1
        slot = slot_of(p, lax.rem(y - sign * (s + 1) + ny, ny), j)
        remote(slot, slot, ys.at[p, way, s, j], yr.at[p, way, s, j], along_y(sign)).wait_recv()

    def ring_step(p, s, pick=None):
        ready = set()
        for i in range(X):
            for way in range(2):
                if s == 0:
                    j = orders[way][0][i]
                    if pick is not None and j not in pick:
                        continue
                    if j not in ready:
                        ready.add(j)
                        if p == 2:
                            if j == 0:
                                local[5].wait()
                            else:
                                e_out[X - j].wait_recv()
                        elif j == 0:
                            local[2 * p].wait()
                            local[2 * p + 1].wait()
                        else:
                            v_out[p, X - j].wait_recv()
                            t_out[p, X - j].wait_recv()
                    sends = True
                else:
                    full = orders[way][min(s, 2)] if s < steps else orders[way][3]
                    if i >= len(full):
                        continue
                    j = full[i]
                    came(p, s - 1, j, way)
                    sends = s < steps and j in orders[way][s]
                if sends:
                    copy = hop(p, s, j, way)
                    copy.start()
                    sent.append(copy)

    def convert_step(p, s):
        convert(p, lax.rem(y + s, ny))
        if 0 < s < steps:
            convert(p, lax.rem(y - s + ny, ny))

    nt, nn = ((1,), (1,)), ((1,), (0,))

    def mine(index):
        return pl.ds(pl.multiple_of(index * piece, 8), piece)

    def products(targets, left, right):
        for ref, _ in targets:
            ref[...] = jnp.zeros_like(ref)

        @pl.loop(0, chunks)
        def _(k):
            cols = pl.ds(pl.multiple_of(k * wide, LANE), wide)
            value = (
                dot_bf16(bhi[left, cols], bhi[right, cols], nt)
                + dot_bf16(bhi[left, cols], blo[right, cols], nt)
                + dot_bf16(blo[left, cols], bhi[right, cols], nt)
            )
            for ref, lo in targets:
                ref[...] += value[lo : lo + LANE]

    started = []

    def scatter_start(p):
        for d in far:
            copy = remote(
                part.at[p, mine(lax.rem(m + d, members))], ra.at[p, d], a_s.at[p, d], a_r.at[p, d], in_group(d)
            )
            copy.start()
            started.append(copy)

    def column_start(p):
        total = part[p, mine(m), :]
        for d in range(1, members):
            remote(part.at[p, mine(m)], ra.at[p, d], a_s.at[p, d], a_r.at[p, d], in_group(d)).wait_recv()
        for d in range(1, members):
            total = total + ra[p, d]
        qsum[p] = total
        for d in far:
            copy = remote(qsum.at[p], rb.at[p, d], b_s.at[p, d], b_r.at[p, d], along_z(d))
            copy.start()
            started.append(copy)

    def spread_start(p):
        total = qsum[p]
        for d in range(1, nz):
            remote(qsum.at[p], rb.at[p, d], b_s.at[p, d], b_r.at[p, d], along_z(d)).wait_recv()
        for d in range(1, nz):
            total = total + rb[p, d]
        rc[p, mine(m), :] = total
        for d in far:
            copy = remote(rc.at[p, mine(m)], rc.at[p, mine(m)], c_s.at[p, d], c_r.at[p, d], in_group(d))
            copy.start()
            started.append(copy)

    def spread_done(p):
        for d in range(1, members):
            theirs = rc.at[p, mine(lax.rem(m + members - d, members))]
            remote(theirs, theirs, c_s.at[p, d], c_r.at[p, d], in_group(d)).wait_recv()

    def scale(p, value):
        hi, lo = split_hi_lo(value)
        yhi[p] = hi
        ylo[p] = lo

    def change(p, cols):
        vectors = pl.ds(X * rows + p * LANE, LANE)
        return (
            dot_bf16(yhi[p], bhi[vectors, cols], nn)
            + dot_bf16(yhi[p], blo[vectors, cols], nn)
            + dot_bf16(ylo[p], bhi[vectors, cols], nn)
        )

    def triangle(p):
        for r in range(ny):
            for k in range(X):
                tmat[p, pl.ds((r * X + k) * 4, 4), :] = vbuf[p, r, k, :, pl.ds(width, LANE)]

    e_out = {}

    def ext_start():
        for d in (1, 3, 2):
            e_out[d] = remote(opposite(lax.rem(x + d, X)), vext.at[y, x], ex_s.at[d], ex_r.at[d], along_x(d))
            e_out[d].start()
            started.append(e_out[d])

    def ext_convert(*which):
        for q in which:
            row = lax.rem(y + items[q] + ny, ny)
            base = pl.multiple_of(row * 16, 16)
            hi, lo = split_hi_lo(jnp.concatenate([vext[row, k] for k in range(X)], axis=0))
            ehi[pl.ds(base, 16), :] = hi
            elo[pl.ds(base, 16), :] = lo

    items = (0, 1, -1, 2, -2, 3, -3, 4)
    sides = (1, 3)
    kept = chunks - LENT
    lent_at, lent = kept * wide, LENT * wide

    def lend(*which):
        for q in which:
            row = lax.rem(y + items[q] + ny, ny)
            for i, d in enumerate(sides):
                copy = remote(
                    vbuf.at[1, row, :, :, pl.ds(lent_at, lent)], pbuf.at[i, row], p_s.at[i, q], p_r.at[i, q], along_x(d)
                )
                copy.start()
                started.append(copy)

    def borrow(*which):
        for q in which:
            row = lax.rem(y + items[q] + ny, ny)
            for i, d in enumerate(sides):
                remote(
                    vbuf.at[1, row, :, :, pl.ds(lent_at, lent)], pbuf.at[i, row], p_s.at[i, q], p_r.at[i, q], along_x(d)
                ).wait_recv()
                base = pl.multiple_of(row * 16, 16)
                hi, lo = split_hi_lo(jnp.concatenate([pbuf[i, row, k] for k in range(X)], axis=0))
                phi[i, pl.ds(base, 16), :] = hi
                plo[i, pl.ds(base, 16), :] = lo

    def far_base(k):
        theirs = pl.ds(pl.multiple_of(lax.rem(x + X // 2, X) * rows, 8), rows)
        at_k = k - (chunks - RING)
        return remote(obuf.at[k, theirs], ebase.at[at_k], eb_s.at[at_k], eb_r.at[at_k], along_x(X // 2))

    def base_copy(k, i):
        theirs = pl.ds(pl.multiple_of(lax.rem(x + sides[i], X) * rows, 8), rows)
        return remote(
            obuf.at[k, theirs], sbase.at[i, k - kept], q_s.at[i, k - kept], q_r.at[i, k - kept], along_x(sides[i])
        )

    ring_step(0, 0, (0,))
    ring_step(1, 0, (0,))
    ring_step(0, 0, (1, 2, 3))
    convert_step(0, 0)
    ring_step(0, 1)
    convert_step(0, 1)
    ring_step(0, 2)
    ring_step(1, 0, (1, 2, 3))
    convert_step(0, 2)
    ring_step(0, 3)
    convert_step(0, 3)
    convert_step(1, 0)
    ring_step(0, 4)
    ring_step(1, 1)
    convert_step(0, 4)
    triangle(0)

    local[4].wait()
    for d in (1, 3, 2):
        s_out[d].wait_recv()
    for k in range(X):
        hi, lo = split_hi_lo(sbuf[k])
        bhi[pl.ds(k * rows, rows), :] = hi
        blo[pl.ds(k * rows, rows), :] = lo
    products([(part.at[0], 0)], pl.ds(0, LANE), pl.ds(LANE, LANE))
    scatter_start(0)
    convert_step(1, 1)
    ext_start()
    lend(0, 1, 2)
    ring_step(1, 2)
    column_start(0)
    convert_step(1, 2)
    lend(3, 4)
    ring_step(1, 3)
    ring_step(2, 0)
    spread_start(0)
    convert_step(1, 3)
    lend(5, 6)
    ring_step(1, 4)
    convert_step(1, 4)
    triangle(1)
    products([(part.at[1], 0), (gram, LANE)], pl.ds(0, 2 * LANE), pl.ds(2 * LANE, LANE))
    ring_step(2, 1)
    spread_done(0)
    upper = dot_f32(rc[0], tmat[0], nt)
    part[1] = part[1] - dot_f32(upper, gram[...], nn)
    scatter_start(1)
    scale(0, upper)

    def first_change(k):
        cols = pl.ds(k * wide, wide)
        value = change(0, cols)
        for q in range(X):
            obuf[k, pl.ds(q * rows, rows), :] = sbuf[q, :, cols] - value[q * rows : (q + 1) * rows]

    lend(7)
    for k in range(chunks - 1, chunks - 1 - max(LENT, RING), -1):
        first_change(k)
        if k >= kept:
            for i in range(2):
                base_copy(k, i).start()
        if k >= chunks - RING:
            far_base(k).start()
    ring_step(2, 2)
    column_start(1)
    ring_step(2, 3)
    for k in range(chunks - max(LENT, RING)):
        first_change(k)
    borrow(0, 1, 2, 3, 4)
    spread_start(1)
    borrow(5, 6, 7)
    ring_step(2, 4)
    ext_convert(*range(len(items)))
    spread_done(1)
    scale(1, dot_f32(rc[1], tmat[1], nt))

    def block(k, d, skip):
        to = lax.rem(x + d, X)
        mine_rows = pl.ds(pl.multiple_of(to * rows, 8), rows)
        src = obuf.at[k, mine_rows, pl.ds(skip, wide - skip)]
        dst = o_hbm.at[:, pl.ds(pl.multiple_of(own_start + k * wide + skip, LANE), wide - skip)]
        return src, dst

    def outward(k):
        return ((2,) if k < chunks - RING else ()) + ((1, 3) if k < kept else ())

    def ship(k, skip):
        for d in outward(k):
            src, dst = block(k, d, skip)
            remote(src, dst, o_s.at[k, d], o_r.at[k, d], along_x(d)).start()
        src, dst = block(k, 0, skip)
        pltpu.make_async_copy(src, dst, o_l.at[k]).start()

    def shipped(k, skip):
        for d in outward(k):
            src, dst = block(k, d, skip)
            remote(src, dst, o_s.at[k, d], o_r.at[k, d], along_x(d)).wait_send()
        src, dst = block(k, 0, skip)
        pltpu.make_async_copy(src, dst, o_l.at[k]).wait()

    def by_width(k, act, where_x):
        if k > 0:
            act(k, 0)
            return

        @pl.when(where_x < 2)
        def _():
            act(k, 0)

        @pl.when(where_x >= 2)
        def _():
            act(k, LANE)

    for k in range(chunks):
        cols = pl.ds(k * wide, wide)
        if k >= kept:
            for i in range(2):
                base_copy(k, i).wait_send()
        if k >= chunks - RING:
            far_base(k).wait_send()
        obuf[k] = obuf[k] - change(1, cols)
        if k > 0:
            by_width(k - 1, ship, x)
    by_width(chunks - 1, ship, x)

    own_rows = pl.ds(pl.multiple_of(x * rows, 16), rows)
    finished = []
    for k in range(RING):
        cols = pl.ds(k * wide, wide)
        far_base(chunks - RING + k).wait_recv()
        ebuf[:, cols] = ebase[k] - (
            dot_bf16(yhi[1, own_rows], ehi[:, cols], nn)
            + dot_bf16(yhi[1, own_rows], elo[:, cols], nn)
            + dot_bf16(ylo[1, own_rows], ehi[:, cols], nn)
        )
    start = quarter_start(lax.rem(x + X // 2, X)) + ext_at
    finished.append(pltpu.make_async_copy(ebuf, o_hbm.at[:, pl.ds(pl.multiple_of(start, LANE), ext)], f_l.at[2]))
    finished[0].start()
    for i in range(2):
        source = lax.rem(x + X - sides[i], X)
        value = (
            dot_bf16(yhi[1, own_rows], phi[i], nn)
            + dot_bf16(yhi[1, own_rows], plo[i], nn)
            + dot_bf16(ylo[1, own_rows], phi[i], nn)
        )
        for k in range(kept, chunks):
            base_copy(k, i).wait_recv()
            part_of = pl.ds((k - kept) * wide, wide)
            fbuf[i, :, part_of] = sbase[i, k - kept] - value[:, (k - kept) * wide : (k - kept + 1) * wide]
        copy = pltpu.make_async_copy(
            fbuf.at[i],
            o_hbm.at[:, pl.ds(pl.multiple_of(quarter_start(source) + lent_at, LANE), lent)],
            f_l.at[i],
        )
        copy.start()
        finished.append(copy)

    for d in (1, 3, 2):
        for p in range(2):
            v_out[p, d].wait_send()
            t_out[p, d].wait_send()
        s_out[d].wait_send()
    for copy in sent + started:
        copy.wait_send()
    for copy in finished:
        copy.wait()
    for k in range(chunks):
        by_width(k, shipped, x)
        for d in outward(k):
            source = lax.rem(x + X - d, X)

            def arrived(k, skip, d=d):
                src, dst = block(k, d, skip)
                remote(src, dst, o_s.at[k, d], o_r.at[k, d], along_x(d)).wait_recv()

            by_width(k, arrived, source)


def solution(mesh):
    ny, nz = mesh.shape["pcol"] // X, mesh.shape["prow"] // 2

    def body(slab, reflectors, factors):
        rows, entries = slab.shape
        width = -(-entries // (X * LANE)) * LANE
        chunks = 5
        wide = width // chunks
        f32, bf16 = jnp.float32, jnp.bfloat16
        vmem, dma = pltpu.VMEM, pltpu.SemaphoreType.DMA
        any_space = pl.BlockSpec(memory_space=pl.ANY)
        return pl.pallas_call(
            functools.partial(kernel, (ny, nz, rows, width, chunks)),
            out_shape=jax.ShapeDtypeStruct(slab.shape, f32),
            in_specs=[any_space] * 3,
            out_specs=any_space,
            scratch_shapes=[
                vmem((2, ny, X, 4, width + LANE), f32),
                vmem((X, rows, width), f32),
                vmem((3 * LANE, width), bf16),
                vmem((3 * LANE, width), bf16),
                vmem((2, LANE, LANE), f32),
                vmem((2, LANE, LANE), f32),
                vmem((LANE, LANE), f32),
                vmem((2, 2 * X, 16, LANE), f32),
                vmem((2, 16, LANE), f32),
                vmem((2, nz, 16, LANE), f32),
                vmem((2, LANE, LANE), f32),
                vmem((2, LANE, LANE), bf16),
                vmem((2, LANE, LANE), bf16),
                vmem((chunks, X * rows, wide), f32),
                vmem((2, ny, X, 4, LENT * wide), f32),
                vmem((2, LANE, LENT * wide), bf16),
                vmem((2, LANE, LENT * wide), bf16),
                vmem((2, LENT, rows, wide), f32),
                vmem((2, rows, LENT * wide), f32),
                vmem((ny, X, 4, RING * wide), f32),
                vmem((LANE, RING * wide), bf16),
                vmem((LANE, RING * wide), bf16),
                vmem((RING, rows, wide), f32),
                vmem((rows, RING * wide), f32),
                dma((2, X)), dma((2, X)), dma((2, X)), dma((2, X)), dma((X,)), dma((X,)),
                dma((6,)),
                dma((3, 2, ny // 2, X)), dma((3, 2, ny // 2, X)),
                dma((2, 2 * X)), dma((2, 2 * X)), dma((2, nz)), dma((2, nz)), dma((2, 2 * X)), dma((2, 2 * X)),
                dma((chunks, X)), dma((chunks, X)), dma((chunks,)),
                dma((2, ny)), dma((2, ny)), dma((2, LENT)), dma((2, LENT)), dma((3,)),
                dma((X,)), dma((X,)), dma((RING,)), dma((RING,)),
            ],
            compiler_params=pltpu.CompilerParams(
                collective_id=0, has_side_effects=True, vmem_limit_bytes=40 << 20
            ),
            name="backtransform",
        )(*(pltpu.with_memory_space_constraint(a, pltpu.HBM) for a in (slab, reflectors, factors)))

    in_specs = (P("pcol", "prow"), P(None, "pcol", "prow"), P(None, "pcol", None))
    return jax.shard_map(body, mesh=mesh, in_specs=in_specs, out_specs=P("pcol", "prow"), check_vma=False)
```

```python
import functools

import jax
import jax.numpy as jnp
from jax import lax
from jax.experimental import pallas as pl
from jax.experimental.pallas import tpu as pltpu
from jax.sharding import PartitionSpec as P

X = 4
MESH = pl.DeviceIdType.MESH
LANE = 128
LENT = 2
RING = 3


def quarter_start(x):
    return pl.multiple_of((24 * x + (x + X - 1) // X) * LANE, LANE)


def dot_f32(left, right, dims):
    return lax.dot_general(
        left, right, (dims, ((), ())), precision=lax.Precision.HIGHEST, preferred_element_type=jnp.float32
    )


def dot_bf16(left, right, dims):
    return lax.dot_general(left, right, (dims, ((), ())), preferred_element_type=jnp.float32)


def split_hi_lo(value):
    hi = value.astype(jnp.bfloat16)
    lo = (value - hi.astype(jnp.float32)).astype(jnp.bfloat16)
    return hi, lo


def kernel(
    dims, s_hbm, v_hbm, t_hbm, o_hbm,
    vbuf, sbuf, bhi, blo, tmat, part, gram, ra, qsum, rb, rc, yhi, ylo, obuf, pbuf, phi, plo, sbase, fbuf, vext, ehi, elo, ebase, ebuf,
    vx_s, vx_r, tx_s, tx_r, sx_s, sx_r, loc, ys, yr, a_s, a_r, b_s, b_r, c_s, c_r, o_s, o_r, o_l, p_s, p_r, q_s, q_r, f_l, ex_s, ex_r, eb_s, eb_r,
):
    ny, nz, rows, width, chunks = dims
    wide = width // chunks
    pr, pc = lax.axis_index("prow"), lax.axis_index("pcol")
    x, y, z, c = lax.rem(pc, X), pc // X, pr // 2, lax.rem(pr, 2)
    m = x * 2 + c
    members = 2 * X
    piece = LANE // members
    far = (4, 3, 5, 2, 6, 1, 7)

    def at(x_to, y_to, z_to, c_to):
        return {"prow": z_to * 2 + c_to, "pcol": y_to * X + x_to}

    def along_x(d):
        return at(lax.rem(x + d, X), y, z, c)

    def along_y(d):
        return at(x, lax.rem(y + d + ny, ny), z, c)

    def along_z(d):
        return at(x, y, lax.rem(z + d, nz), c)

    def in_group(d):
        to = lax.rem(m + d, members)
        return at(to // 2, y, z, lax.rem(to, 2))

    def remote(src, dst, send, recv, to):
        return pltpu.make_async_remote_copy(
            src_ref=src, dst_ref=dst, send_sem=send, recv_sem=recv, device_id=to, device_id_type=MESH
        )

    own_start = quarter_start(x)
    local = []
    for p in range(2):
        local.append(
            pltpu.make_async_copy(
                v_hbm.at[p, :, pl.ds(own_start, width)], vbuf.at[p, y, x, :, pl.ds(0, width)], loc.at[p]
            )
        )
        local.append(pltpu.make_async_copy(t_hbm.at[p], vbuf.at[p, y, x, :, pl.ds(width, LANE)], loc.at[2 + p]))
    local.append(pltpu.make_async_copy(s_hbm.at[:, pl.ds(own_start, width)], sbuf.at[x], loc.at[4]))
    ext, ext_at = RING * wide, (chunks - RING) * wide

    def opposite(x_of):
        start = quarter_start(lax.rem(x_of + X // 2, X)) + ext_at
        return v_hbm.at[1, :, pl.ds(pl.multiple_of(start, LANE), ext)]

    local.append(pltpu.make_async_copy(opposite(x), vext.at[y, x], loc.at[5]))
    for copy in local:
        copy.start()

    barrier = pltpu.get_barrier_semaphore()
    peers = [along_y(1), along_y(-1)] + [in_group(d) for d in range(1, members)] + [along_z(d) for d in range(1, nz)]
    for to in peers:
        pl.semaphore_signal(barrier, inc=1, device_id=to, device_id_type=MESH)
    pl.semaphore_wait(barrier, len(peers))

    v_out, t_out, s_out = {}, {}, {}
    for p in range(2):
        for d in (1, 3, 2):
            start = quarter_start(lax.rem(x + d, X))
            v_out[p, d] = remote(
                v_hbm.at[p, :, pl.ds(start, width)], vbuf.at[p, y, x, :, pl.ds(0, width)],
                vx_s.at[p, d], vx_r.at[p, d], along_x(d),
            )
            t_out[p, d] = remote(
                t_hbm.at[p], vbuf.at[p, y, x, :, pl.ds(width, LANE)], tx_s.at[p, d], tx_r.at[p, d], along_x(d)
            )
            v_out[p, d].start()
            t_out[p, d].start()
    for d in (1, 3, 2):
        start = quarter_start(lax.rem(x + d, X))
        s_out[d] = remote(s_hbm.at[:, pl.ds(start, width)], sbuf.at[x], sx_s.at[d], sx_r.at[d], along_x(d))
        s_out[d].start()

    def convert(p, row):
        keep = jnp.where(x < 2, 1.0, 0.0)
        base = pl.multiple_of(X * rows + p * LANE + row * 16, 16)
        value = jnp.concatenate([vbuf[p, row, k, :, pl.ds(0, width)] for k in range(X)], axis=0)
        value = jnp.concatenate([value[:, :LANE] * keep, value[:, LANE:]], axis=1)
        hi, lo = split_hi_lo(value)
        bhi[pl.ds(base, 16), :] = hi
        blo[pl.ds(base, 16), :] = lo

    steps = ny // 2
    orders = (((0, 1, 3, 2),) * 3 + ((0, 1),), ((0, 3, 1, 2), (3, 0, 2, 1), (3, 2, 0, 1), (3, 2)))
    sent = []

    def slot_of(p, row, j):
        from_x = lax.rem(x + j, X)
        return vext.at[row, from_x] if p == 2 else vbuf.at[p, row, from_x]

    def hop(p, s, j, way):
        sign = 1 if way == 0 else -1
        slot = slot_of(p, lax.rem(y - sign * s + ny, ny), j)
        return remote(slot, slot, ys.at[p, way, s, j], yr.at[p, way, s, j], along_y(sign))

    def came(p, s, j, way):
        sign = 1 if way == 0 else -1
        slot = slot_of(p, lax.rem(y - sign * (s + 1) + ny, ny), j)
        remote(slot, slot, ys.at[p, way, s, j], yr.at[p, way, s, j], along_y(sign)).wait_recv()

    def ring_step(p, s, pick=None):
        ready = set()
        for i in range(X):
            for way in range(2):
                if s == 0:
                    j = orders[way][0][i]
                    if pick is not None and j not in pick:
                        continue
                    if j not in ready:
                        ready.add(j)
                        if p == 2:
                            if j == 0:
                                local[5].wait()
                            else:
                                e_out[X - j].wait_recv()
                        elif j == 0:
                            local[2 * p].wait()
                            local[2 * p + 1].wait()
                        else:
                            v_out[p, X - j].wait_recv()
                            t_out[p, X - j].wait_recv()
                    sends = True
                else:
                    full = orders[way][min(s, 2)] if s < steps else orders[way][3]
                    if i >= len(full):
                        continue
                    j = full[i]
                    came(p, s - 1, j, way)
                    sends = s < steps and j in orders[way][s]
                if sends:
                    copy = hop(p, s, j, way)
                    copy.start()
                    sent.append(copy)

    def convert_step(p, s):
        convert(p, lax.rem(y + s, ny))
        if 0 < s < steps:
            convert(p, lax.rem(y - s + ny, ny))

    nt, nn = ((1,), (1,)), ((1,), (0,))

    def mine(index):
        return pl.ds(pl.multiple_of(index * piece, 8), piece)

    def products(targets, left, right):
        for ref, _ in targets:
            ref[...] = jnp.zeros_like(ref)

        @pl.loop(0, chunks)
        def _(k):
            cols = pl.ds(pl.multiple_of(k * wide, LANE), wide)
            value = (
                dot_bf16(bhi[left, cols], bhi[right, cols], nt)
                + dot_bf16(bhi[left, cols], blo[right, cols], nt)
                + dot_bf16(blo[left, cols], bhi[right, cols], nt)
            )
            for ref, lo in targets:
                ref[...] += value[lo : lo + LANE]

    started = []

    def scatter_start(p):
        for d in far:
            copy = remote(
                part.at[p, mine(lax.rem(m + d, members))], ra.at[p, d], a_s.at[p, d], a_r.at[p, d], in_group(d)
            )
            copy.start()
            started.append(copy)

    def column_start(p):
        total = part[p, mine(m), :]
        for d in range(1, members):
            remote(part.at[p, mine(m)], ra.at[p, d], a_s.at[p, d], a_r.at[p, d], in_group(d)).wait_recv()
        for d in range(1, members):
            total = total + ra[p, d]
        qsum[p] = total
        for d in far:
            copy = remote(qsum.at[p], rb.at[p, d], b_s.at[p, d], b_r.at[p, d], along_z(d))
            copy.start()
            started.append(copy)

    def spread_start(p):
        total = qsum[p]
        for d in range(1, nz):
            remote(qsum.at[p], rb.at[p, d], b_s.at[p, d], b_r.at[p, d], along_z(d)).wait_recv()
        for d in range(1, nz):
            total = total + rb[p, d]
        rc[p, mine(m), :] = total
        for d in far:
            copy = remote(rc.at[p, mine(m)], rc.at[p, mine(m)], c_s.at[p, d], c_r.at[p, d], in_group(d))
            copy.start()
            started.append(copy)

    def spread_done(p):
        for d in range(1, members):
            theirs = rc.at[p, mine(lax.rem(m + members - d, members))]
            remote(theirs, theirs, c_s.at[p, d], c_r.at[p, d], in_group(d)).wait_recv()

    def scale(p, value):
        hi, lo = split_hi_lo(value)
        yhi[p] = hi
        ylo[p] = lo

    def change(p, cols):
        vectors = pl.ds(X * rows + p * LANE, LANE)
        return (
            dot_bf16(yhi[p], bhi[vectors, cols], nn)
            + dot_bf16(yhi[p], blo[vectors, cols], nn)
            + dot_bf16(ylo[p], bhi[vectors, cols], nn)
        )

    def triangle(p):
        for r in range(ny):
            for k in range(X):
                tmat[p, pl.ds((r * X + k) * 4, 4), :] = vbuf[p, r, k, :, pl.ds(width, LANE)]

    e_out = {}

    def ext_start():
        for d in (1, 3, 2):
            e_out[d] = remote(opposite(lax.rem(x + d, X)), vext.at[y, x], ex_s.at[d], ex_r.at[d], along_x(d))
            e_out[d].start()
            started.append(e_out[d])

    def ext_convert(*which):
        for q in which:
            row = lax.rem(y + items[q] + ny, ny)
            base = pl.multiple_of(row * 16, 16)
            hi, lo = split_hi_lo(jnp.concatenate([vext[row, k] for k in range(X)], axis=0))
            ehi[pl.ds(base, 16), :] = hi
            elo[pl.ds(base, 16), :] = lo

    items = (0, 1, -1, 2, -2, 3, -3, 4)
    sides = (1, 3)
    kept = chunks - LENT
    lent_at, lent = kept * wide, LENT * wide

    def lend(*which):
        for q in which:
            row = lax.rem(y + items[q] + ny, ny)
            for i, d in enumerate(sides):
                copy = remote(
                    vbuf.at[1, row, :, :, pl.ds(lent_at, lent)], pbuf.at[i, row], p_s.at[i, q], p_r.at[i, q], along_x(d)
                )
                copy.start()
                started.append(copy)

    def borrow(*which):
        for q in which:
            row = lax.rem(y + items[q] + ny, ny)
            for i, d in enumerate(sides):
                remote(
                    vbuf.at[1, row, :, :, pl.ds(lent_at, lent)], pbuf.at[i, row], p_s.at[i, q], p_r.at[i, q], along_x(d)
                ).wait_recv()
                base = pl.multiple_of(row * 16, 16)
                hi, lo = split_hi_lo(jnp.concatenate([pbuf[i, row, k] for k in range(X)], axis=0))
                phi[i, pl.ds(base, 16), :] = hi
                plo[i, pl.ds(base, 16), :] = lo

    def far_base(k):
        theirs = pl.ds(pl.multiple_of(lax.rem(x + X // 2, X) * rows, 8), rows)
        at_k = k - (chunks - RING)
        return remote(obuf.at[k, theirs], ebase.at[at_k], eb_s.at[at_k], eb_r.at[at_k], along_x(X // 2))

    def base_copy(k, i):
        theirs = pl.ds(pl.multiple_of(lax.rem(x + sides[i], X) * rows, 8), rows)
        return remote(
            obuf.at[k, theirs], sbase.at[i, k - kept], q_s.at[i, k - kept], q_r.at[i, k - kept], along_x(sides[i])
        )

    ring_step(0, 0, (0,))
    ring_step(1, 0, (0,))
    ring_step(0, 0, (1, 2, 3))
    convert_step(0, 0)
    ring_step(0, 1)
    convert_step(0, 1)
    ring_step(0, 2)
    ring_step(1, 0, (1, 2, 3))
    convert_step(0, 2)
    ring_step(0, 3)
    convert_step(0, 3)
    convert_step(1, 0)
    ring_step(0, 4)
    ring_step(1, 1)
    convert_step(0, 4)
    triangle(0)

    for j in (0, 3, 1, 2):
        if j == 0:
            local[4].wait()
        else:
            s_out[X - j].wait_recv()
        k = lax.rem(x + j, X)
        base = pl.ds(pl.multiple_of(k * rows, 16), rows)
        hi, lo = split_hi_lo(sbuf[k])
        bhi[base, :] = hi
        blo[base, :] = lo
    products([(part.at[0], 0)], pl.ds(0, LANE), pl.ds(LANE, LANE))
    scatter_start(0)
    convert_step(1, 1)
    ext_start()
    lend(0, 1, 2)
    ring_step(1, 2)
    column_start(0)
    convert_step(1, 2)
    lend(3, 4)
    ring_step(1, 3)
    ring_step(2, 0)
    spread_start(0)
    convert_step(1, 3)
    lend(5, 6)
    ring_step(1, 4)
    convert_step(1, 4)
    triangle(1)
    products([(part.at[1], 0), (gram, LANE)], pl.ds(0, 2 * LANE), pl.ds(2 * LANE, LANE))
    ring_step(2, 1)
    spread_done(0)
    upper = dot_f32(rc[0], tmat[0], nt)
    part[1] = part[1] - dot_f32(upper, gram[...], nn)
    scatter_start(1)
    scale(0, upper)

    def first_change(k):
        cols = pl.ds(k * wide, wide)
        value = change(0, cols)
        for q in range(X):
            obuf[k, pl.ds(q * rows, rows), :] = sbuf[q, :, cols] - value[q * rows : (q + 1) * rows]

    lend(7)
    for k in range(chunks - 1, chunks - 1 - max(LENT, RING), -1):
        first_change(k)
        if k >= kept:
            for i in range(2):
                base_copy(k, i).start()
        if k >= chunks - RING:
            far_base(k).start()
    column_start(1)
    ring_step(2, 2)
    for k in range(chunks - max(LENT, RING)):
        first_change(k)
    borrow(0, 1, 2, 3, 4)
    spread_start(1)
    ring_step(2, 3)
    borrow(5, 6, 7)
    spread_done(1)
    scale(1, dot_f32(rc[1], tmat[1], nt))

    def block(k, d, skip):
        to = lax.rem(x + d, X)
        mine_rows = pl.ds(pl.multiple_of(to * rows, 8), rows)
        src = obuf.at[k, mine_rows, pl.ds(skip, wide - skip)]
        dst = o_hbm.at[:, pl.ds(pl.multiple_of(own_start + k * wide + skip, LANE), wide - skip)]
        return src, dst

    def outward(k):
        return ((2,) if k < chunks - RING else ()) + ((1, 3) if k < kept else ())

    def ship(k, skip):
        for d in outward(k):
            src, dst = block(k, d, skip)
            remote(src, dst, o_s.at[k, d], o_r.at[k, d], along_x(d)).start()
        src, dst = block(k, 0, skip)
        pltpu.make_async_copy(src, dst, o_l.at[k]).start()

    def shipped(k, skip):
        for d in outward(k):
            src, dst = block(k, d, skip)
            remote(src, dst, o_s.at[k, d], o_r.at[k, d], along_x(d)).wait_send()
        src, dst = block(k, 0, skip)
        pltpu.make_async_copy(src, dst, o_l.at[k]).wait()

    def by_width(k, act, where_x):
        if k > 0:
            act(k, 0)
            return

        @pl.when(where_x < 2)
        def _():
            act(k, 0)

        @pl.when(where_x >= 2)
        def _():
            act(k, LANE)

    for k in range(chunks):
        cols = pl.ds(k * wide, wide)
        if k >= kept:
            for i in range(2):
                base_copy(k, i).wait_send()
        if k >= chunks - RING:
            far_base(k).wait_send()
        obuf[k] = obuf[k] - change(1, cols)
        by_width(k, ship, x)

    ring_step(2, 4)
    ext_convert(*range(len(items)))
    own_rows = pl.ds(pl.multiple_of(x * rows, 16), rows)
    finished = []
    for k in range(RING):
        cols = pl.ds(k * wide, wide)
        far_base(chunks - RING + k).wait_recv()
        ebuf[:, cols] = ebase[k] - (
            dot_bf16(yhi[1, own_rows], ehi[:, cols], nn)
            + dot_bf16(yhi[1, own_rows], elo[:, cols], nn)
            + dot_bf16(ylo[1, own_rows], ehi[:, cols], nn)
        )
    start = quarter_start(lax.rem(x + X // 2, X)) + ext_at
    finished.append(pltpu.make_async_copy(ebuf, o_hbm.at[:, pl.ds(pl.multiple_of(start, LANE), ext)], f_l.at[2]))
    finished[0].start()
    for i in range(2):
        source = lax.rem(x + X - sides[i], X)
        value = (
            dot_bf16(yhi[1, own_rows], phi[i], nn)
            + dot_bf16(yhi[1, own_rows], plo[i], nn)
            + dot_bf16(ylo[1, own_rows], phi[i], nn)
        )
        for k in range(kept, chunks):
            base_copy(k, i).wait_recv()
            part_of = pl.ds((k - kept) * wide, wide)
            fbuf[i, :, part_of] = sbase[i, k - kept] - value[:, (k - kept) * wide : (k - kept + 1) * wide]
        copy = pltpu.make_async_copy(
            fbuf.at[i],
            o_hbm.at[:, pl.ds(pl.multiple_of(quarter_start(source) + lent_at, LANE), lent)],
            f_l.at[i],
        )
        copy.start()
        finished.append(copy)

    for d in (1, 3, 2):
        for p in range(2):
            v_out[p, d].wait_send()
            t_out[p, d].wait_send()
        s_out[d].wait_send()
    for copy in sent + started:
        copy.wait_send()
    for copy in finished:
        copy.wait()
    for k in range(chunks):
        by_width(k, shipped, x)
        for d in outward(k):
            source = lax.rem(x + X - d, X)

            def arrived(k, skip, d=d):
                src, dst = block(k, d, skip)
                remote(src, dst, o_s.at[k, d], o_r.at[k, d], along_x(d)).wait_recv()

            by_width(k, arrived, source)


def solution(mesh):
    ny, nz = mesh.shape["pcol"] // X, mesh.shape["prow"] // 2

    def body(slab, reflectors, factors):
        rows, entries = slab.shape
        width = -(-entries // (X * LANE)) * LANE
        chunks = 5
        wide = width // chunks
        f32, bf16 = jnp.float32, jnp.bfloat16
        vmem, dma = pltpu.VMEM, pltpu.SemaphoreType.DMA
        any_space = pl.BlockSpec(memory_space=pl.ANY)
        return pl.pallas_call(
            functools.partial(kernel, (ny, nz, rows, width, chunks)),
            out_shape=jax.ShapeDtypeStruct(slab.shape, f32),
            in_specs=[any_space] * 3,
            out_specs=any_space,
            scratch_shapes=[
                vmem((2, ny, X, 4, width + LANE), f32),
                vmem((X, rows, width), f32),
                vmem((3 * LANE, width), bf16),
                vmem((3 * LANE, width), bf16),
                vmem((2, LANE, LANE), f32),
                vmem((2, LANE, LANE), f32),
                vmem((LANE, LANE), f32),
                vmem((2, 2 * X, 16, LANE), f32),
                vmem((2, 16, LANE), f32),
                vmem((2, nz, 16, LANE), f32),
                vmem((2, LANE, LANE), f32),
                vmem((2, LANE, LANE), bf16),
                vmem((2, LANE, LANE), bf16),
                vmem((chunks, X * rows, wide), f32),
                vmem((2, ny, X, 4, LENT * wide), f32),
                vmem((2, LANE, LENT * wide), bf16),
                vmem((2, LANE, LENT * wide), bf16),
                vmem((2, LENT, rows, wide), f32),
                vmem((2, rows, LENT * wide), f32),
                vmem((ny, X, 4, RING * wide), f32),
                vmem((LANE, RING * wide), bf16),
                vmem((LANE, RING * wide), bf16),
                vmem((RING, rows, wide), f32),
                vmem((rows, RING * wide), f32),
                dma((2, X)), dma((2, X)), dma((2, X)), dma((2, X)), dma((X,)), dma((X,)),
                dma((6,)),
                dma((3, 2, ny // 2, X)), dma((3, 2, ny // 2, X)),
                dma((2, 2 * X)), dma((2, 2 * X)), dma((2, nz)), dma((2, nz)), dma((2, 2 * X)), dma((2, 2 * X)),
                dma((chunks, X)), dma((chunks, X)), dma((chunks,)),
                dma((2, ny)), dma((2, ny)), dma((2, LENT)), dma((2, LENT)), dma((3,)),
                dma((X,)), dma((X,)), dma((RING,)), dma((RING,)),
            ],
            compiler_params=pltpu.CompilerParams(
                collective_id=0, has_side_effects=True, vmem_limit_bytes=40 << 20
            ),
            name="backtransform",
        )(*(pltpu.with_memory_space_constraint(a, pltpu.HBM) for a in (slab, reflectors, factors)))

    in_specs = (P("pcol", "prow"), P(None, "pcol", "prow"), P(None, "pcol", None))
    return jax.shard_map(body, mesh=mesh, in_specs=in_specs, out_specs=P("pcol", "prow"), check_vma=False)
```
